512 devices in a mesh: grid: 32 (over x, y, core), band: 16 (over z).
Axes of the slice: x: 4, y: 4, z: 16, core: 2. Of those that a mesh axis runs over, the one named last changes fastest.
Arguments:
- orbitals: bfloat16 [32768, 512], P('grid', 'band'), may hold values from -6 to 6
- rotation: bfloat16 [512, 32768], P('grid', 'band'), may hold values from -0.25 to 0.25
Outputs:
- rotated: bfloat16 [32768, 32768], P('grid', 'band')
The draws below stay inside these ranges and needn't reach their ends.
All inputs are finite; a program needn't handle non-finite values.
Results may differ from the reference program's by a relative error of at most 0.001.
Values may be sent and summed in bfloat16 or wider, within the bound.
No kernel may reach another device: no remote copies, remote signals or barrier semaphores. Data moves between devices by JAX's collectives and lax.ppermute only.
A program may use at most 64 MiB of HBM per device.

```python
import jax
import jax.numpy as jnp

NB = 32768
KIN = 512
POINTS = 32768


def levels(stream_key, shape, pieces, low, largest):
    level = 1.0
    for position, shards_of in pieces:
        steps = jax.random.uniform(jax.random.fold_in(jax.random.fold_in(stream_key, 6), position), (shards_of,), jnp.float32, low / len(pieces), largest / len(pieces))
        level = level * jnp.repeat(jnp.exp(steps), shape[position] // shards_of).reshape((-1,) + (1,) * (len(shape) - 1 - position))
    return level


def scatter_about(rng, shape, deviation, reach, shards=(), held_as=jnp.bfloat16):
    result = deviation * jax.random.normal(rng, shape, jnp.float32)
    if shards:
        result = result * levels(rng, shape, shards, -0.22, 0.18)
    return jnp.clip(result, -reach, reach).astype(held_as)


def setup_inputs(seed: int = 0) -> dict:
    streams_of = jax.random.split(jax.random.key(seed), 3)
    return {
        "orbitals": scatter_about(streams_of[0], (POINTS, KIN), 1.0, 6.0, ((0, 32), (1, 16))),
        "rotation": scatter_about(streams_of[1], (KIN, NB), KIN ** -0.5, 0.25, ((0, 32), (1, 16))),
    }


def reference(orbitals, rotation):
    product = jnp.dot(orbitals, rotation, preferred_element_type=jnp.float32)
    return product.astype(jnp.bfloat16)
```

```python
import jax
import jax.numpy as jnp
from jax import lax
from jax.sharding import PartitionSpec as P

ALONE = 896


def spread(block, axis):
    n = lax.axis_size(axis)
    copies = jnp.broadcast_to(block[None], (n, *block.shape))
    return lax.all_to_all(copies, axis, 0, 0, tiled=True).reshape(-1, block.shape[1])


def on_device(orbitals, rotation):
    columns = orbitals.T
    all_rows = spread(rotation, "grid")
    rest = spread(columns[:, ALONE:], "band")
    main = lax.all_gather(columns[:, :ALONE], "band", axis=0, tiled=True)
    all_cols = jnp.concatenate([main, rest], axis=1)
    total = lax.dot_general(
        all_cols, all_rows, (((0,), (0,)), ((), ())), preferred_element_type=jnp.float32
    )
    return total.astype(jnp.bfloat16)


def solution(mesh):
    in_specs = (P("grid", "band"), P("grid", "band"))
    out_specs = P("grid", "band")
    return jax.shard_map(
        on_device, mesh=mesh, in_specs=in_specs, out_specs=out_specs, check_vma=False
    )
```

```python
import jax
import jax.numpy as jnp
from jax import lax
from jax.experimental import pallas as pl
from jax.experimental.pallas import tpu as pltpu
from jax.sharding import Mesh
from jax.sharding import PartitionSpec as P

GRID = ("x", "y", "core")
PAIRS, PARITY = "pairs", "parity"
BAND = (PAIRS, PARITY)
VMEM = pl.BlockSpec(memory_space=pltpu.VMEM)
TILE = 512


def params(mib):
    return pltpu.CompilerParams(vmem_limit_bytes=mib << 20)


def copies_of(block, n):
    def kernel(block_ref, out_ref):
        held = block_ref[...]
        for i in range(n):
            out_ref[i] = held

    return pl.pallas_call(
        kernel,
        out_shape=jax.ShapeDtypeStruct((n, *block.shape), block.dtype),
        in_specs=[VMEM],
        out_specs=VMEM,
        compiler_params=params(8),
    )(block)


def turned(cols):
    k, points = cols.shape
    half = points // 2

    def kernel(cols_ref, upper_ref, lower_ref):
        for i in range(0, half, 128):
            upper_ref[i : i + 128, :] = cols_ref[:, i : i + 128].T
            lower_ref[i : i + 128, :] = cols_ref[:, half + i : half + i + 128].T

    shape = jax.ShapeDtypeStruct((half, k), cols.dtype)
    return pl.pallas_call(
        kernel,
        out_shape=(shape, shape),
        in_specs=[VMEM],
        out_specs=(VMEM, VMEM),
        compiler_params=params(8),
    )(cols)


def first_sum(upper, lower, rows):
    half, k = upper.shape
    n = rows.shape[1]

    def kernel(upper_ref, lower_ref, rows_ref, sum_ref):
        for h, part in enumerate((upper_ref, lower_ref)):
            for c in range(0, n, TILE):
                sum_ref[h * half : (h + 1) * half, c : c + TILE] = jnp.dot(
                    part[...],
                    rows_ref[:, c : c + TILE],
                    preferred_element_type=jnp.float32,
                )

    return pl.pallas_call(
        kernel,
        out_shape=jax.ShapeDtypeStruct((2 * half, n), jnp.float32),
        in_specs=[VMEM] * 3,
        out_specs=VMEM,
        compiler_params=params(12),
        cost_estimate=pl.CostEstimate(
            flops=4 * half * k * n, bytes_accessed=8 * half * n, transcendentals=0
        ),
    )(upper, lower, rows)


def finished(total, upper, lower, rows):
    half, k = upper.shape
    n = rows.shape[1]
    tiles = [(h, c) for h in range(2) for c in range(0, n, TILE)]

    def kernel(total_ref, upper_ref, lower_ref, rows_ref, out_ref, held, sems):
        copies = []
        for t, (h, c) in enumerate(tiles):
            part = (upper_ref, lower_ref)[h]
            where = (slice(h * half, (h + 1) * half), slice(c, c + TILE))
            held[t] = (
                total_ref[where]
                + jnp.dot(
                    part[...],
                    rows_ref[:, c : c + TILE],
                    preferred_element_type=jnp.float32,
                )
            ).astype(jnp.bfloat16)
            copies.append(
                pltpu.make_async_copy(held.at[t], out_ref.at[where], sems.at[t])
            )
            copies[-1].start()
        for copy in copies:
            copy.wait()

    return pl.pallas_call(
        kernel,
        out_shape=jax.ShapeDtypeStruct((2 * half, n), jnp.bfloat16),
        in_specs=[VMEM] * 4,
        out_specs=pl.BlockSpec(memory_space=pl.ANY),
        scratch_shapes=[
            pltpu.VMEM((len(tiles), half, TILE), jnp.bfloat16),
            pltpu.SemaphoreType.DMA((len(tiles),)),
        ],
        compiler_params=params(24),
        cost_estimate=pl.CostEstimate(
            flops=4 * half * k * n, bytes_accessed=12 * half * n, transcendentals=0
        ),
    )(total, upper, lower, rows)


def from_band(block, offset):
    n = lax.axis_size(BAND)
    return lax.ppermute(block, BAND, [((i + offset) % n, i) for i in range(n)])


def on_device(orbitals, rotation):
    cols = orbitals.T
    width, n = cols.shape[0], rotation.shape[1]
    sent = copies_of(rotation, lax.axis_size(GRID))
    all_rows = lax.all_to_all(sent, GRID, 0, 0, tiled=True).reshape(-1, 2, width, n)
    parity = lax.axis_index(PARITY)

    def rows(which):
        return lax.dynamic_index_in_dim(all_rows, which, 1, False).reshape(-1, n)

    same = lax.all_gather(cols, PAIRS, axis=0, tiled=True)
    upper, lower = turned(same)
    above = from_band(upper, 1)
    below = from_band(lower, -1)
    total = first_sum(upper, lower, rows(parity))
    return finished(total, above, below, rows(1 - parity))


def solution(mesh):
    n_grid, n_band = mesh.devices.shape
    fine = Mesh(
        mesh.devices.reshape(4, 4, n_grid // 16, n_band // 2, 2), (*GRID, *BAND)
    )
    spec = P(GRID, BAND)
    return jax.shard_map(
        on_device, mesh=fine, in_specs=(spec, spec), out_specs=spec, check_vma=False
    )
```

```python
import jax
import jax.numpy as jnp
from jax import lax
from jax.experimental import pallas as pl
from jax.experimental.pallas import tpu as pltpu
from jax.sharding import Mesh
from jax.sharding import PartitionSpec as P

GRID = ("x", "y", "core")
FAR, NEAR = "far", "near"
BAND = (FAR, NEAR)
VMEM = pl.BlockSpec(memory_space=pltpu.VMEM)
TILE = 512
CUT = 384


def params(mib):
    return pltpu.CompilerParams(vmem_limit_bytes=mib << 20)


def copies_of(block, n):
    held_n = n // 4

    def kernel(block_ref, out_ref, held, sems):
        value = block_ref[...]
        for i in range(held_n):
            held[i] = value
        copies = [
            pltpu.make_async_copy(
                held, out_ref.at[i * held_n : (i + 1) * held_n], sems.at[i]
            )
            for i in range(4)
        ]
        for copy in copies:
            copy.start()
        for copy in copies:
            copy.wait()

    return pl.pallas_call(
        kernel,
        out_shape=jax.ShapeDtypeStruct((n, *block.shape), block.dtype),
        in_specs=[VMEM],
        out_specs=pl.BlockSpec(memory_space=pltpu.HBM),
        scratch_shapes=[
            pltpu.VMEM((held_n, *block.shape), block.dtype),
            pltpu.SemaphoreType.DMA((4,)),
        ],
        compiler_params=params(4),
    )(block)


def turned(cols):
    k, points = cols.shape

    def kernel(cols_ref, out_ref):
        for i in range(0, points, 128):
            out_ref[i : i + 128, :] = cols_ref[:, i : i + 128].T

    return pl.pallas_call(
        kernel,
        out_shape=jax.ShapeDtypeStruct((points, k), cols.dtype),
        in_specs=[VMEM],
        out_specs=VMEM,
        compiler_params=params(8),
    )(cols)


def both(refs, rows, cols=slice(None), axis=1):
    return jnp.concatenate([r[rows, cols] for r in refs], axis=axis)


def first_sum(own, above, own_rows, above_rows):
    points, k = own.shape
    n = own_rows.shape[1]
    half = points // 2

    def kernel(own_ref, above_ref, own_rows_ref, above_rows_ref, sum_ref):
        for p in range(0, points, half):
            at = slice(p, p + half)
            left = both((own_ref, above_ref), at)
            for c in range(0, n, TILE):
                right = both(
                    (own_rows_ref, above_rows_ref), slice(None), slice(c, c + TILE), 0
                )
                sum_ref[at, c : c + TILE] = jnp.dot(
                    left, right, preferred_element_type=jnp.float32
                )

    return pl.pallas_call(
        kernel,
        out_shape=jax.ShapeDtypeStruct((points, n), jnp.float32),
        in_specs=[VMEM] * 4,
        out_specs=VMEM,
        compiler_params=params(12),
        cost_estimate=pl.CostEstimate(
            flops=4 * points * k * n, bytes_accessed=4 * points * n, transcendentals=0
        ),
    )(own, above, own_rows, above_rows)


def finished(total, below, upper, lower, below_rows, across_rows):
    points, k = below.shape
    n = below_rows.shape[1]
    tiles = [(h, c) for h in range(2) for c in range(0, n, TILE)]

    def kernel(
        total_ref, below_ref, upper_ref, lower_ref, below_rows_ref, across_rows_ref,
        out_ref, held, sems,
    ):
        copies = []
        for t, (h, c) in enumerate(tiles):
            at = (slice(0, CUT), slice(CUT, points))[h]
            where = (at, slice(c, c + TILE))
            left = jnp.concatenate(
                [below_ref[at, :], (upper_ref, lower_ref)[h][...]], axis=1
            )
            right = both((below_rows_ref, across_rows_ref), slice(None), where[1], 0)
            held[where] = (
                total_ref[where]
                + jnp.dot(left, right, preferred_element_type=jnp.float32)
            ).astype(jnp.bfloat16)
            copies.append(
                pltpu.make_async_copy(held.at[where], out_ref.at[where], sems.at[t])
            )
            copies[-1].start()
        for copy in copies:
            copy.wait()

    return pl.pallas_call(
        kernel,
        out_shape=jax.ShapeDtypeStruct((points, n), jnp.bfloat16),
        in_specs=[VMEM] * 6,
        out_specs=pl.BlockSpec(memory_space=pl.ANY),
        scratch_shapes=[
            pltpu.VMEM((points, n), jnp.bfloat16),
            pltpu.SemaphoreType.DMA((len(tiles),)),
        ],
        compiler_params=params(24),
        cost_estimate=pl.CostEstimate(
            flops=4 * points * k * n, bytes_accessed=6 * points * n, transcendentals=0
        ),
    )(total, below, upper, lower, below_rows, across_rows)


def from_band(block, offset):
    n = lax.axis_size(BAND)
    return lax.ppermute(block, BAND, [((i + offset) % n, i) for i in range(n)])


def on_device(orbitals, rotation):
    cols = orbitals.T
    width, n = cols.shape[0], rotation.shape[1]
    sent = copies_of(rotation, lax.axis_size(GRID))
    all_rows = lax.all_to_all(sent, GRID, 0, 0, tiled=True)
    all_rows = all_rows.reshape(-1, lax.axis_size(NEAR), width, n)
    near = lax.axis_index(NEAR)

    def rows(offset):
        which = lax.rem(near + offset, lax.axis_size(NEAR))
        return lax.dynamic_index_in_dim(all_rows, which, 1, False).reshape(-1, n)

    whole = turned(lax.all_gather(cols, FAR, axis=0, tiled=True))
    above = from_band(whole, 1)
    below = from_band(whole, -1)
    upper = from_band(above[:CUT], 1)
    lower = from_band(below[CUT:], -1)
    total = first_sum(whole, above, rows(0), rows(1))
    return finished(total, below, upper, lower, rows(3), rows(2))


def solution(mesh):
    n_grid, n_band = mesh.devices.shape
    fine = Mesh(
        mesh.devices.reshape(4, 4, n_grid // 16, n_band // 4, 4), (*GRID, *BAND)
    )
    spec = P(GRID, BAND)
    return jax.shard_map(
        on_device, mesh=fine, in_specs=(spec, spec), out_specs=spec, check_vma=False
    )
```

```python
import jax
import jax.numpy as jnp
from jax import lax
from jax.experimental import pallas as pl
from jax.experimental.pallas import tpu as pltpu
from jax.sharding import Mesh
from jax.sharding import PartitionSpec as P

GRID = ("x", "y", "core")
FAR, NEAR = "far", "near"
BAND = (FAR, NEAR)
VMEM = pl.BlockSpec(memory_space=pltpu.VMEM)
TILE = 512
CUT = 256


def params(mib):
    return pltpu.CompilerParams(vmem_limit_bytes=mib << 20)


def copies_of(block, n):
    held_n = n // 4

    def kernel(block_ref, out_ref, held, sems):
        value = block_ref[...]
        for i in range(held_n):
            held[i] = value
        copies = [
            pltpu.make_async_copy(
                held, out_ref.at[i * held_n : (i + 1) * held_n], sems.at[i]
            )
            for i in range(4)
        ]
        for copy in copies:
            copy.start()
        for copy in copies:
            copy.wait()

    return pl.pallas_call(
        kernel,
        out_shape=jax.ShapeDtypeStruct((n, *block.shape), block.dtype),
        in_specs=[VMEM],
        out_specs=pl.BlockSpec(memory_space=pltpu.HBM),
        scratch_shapes=[
            pltpu.VMEM((held_n, *block.shape), block.dtype),
            pltpu.SemaphoreType.DMA((4,)),
        ],
        compiler_params=params(4),
    )(block)


def turned(cols):
    k, points = cols.shape

    def kernel(cols_ref, out_ref):
        for i in range(0, points, 128):
            out_ref[i : i + 128, :] = cols_ref[:, i : i + 128].T

    return pl.pallas_call(
        kernel,
        out_shape=jax.ShapeDtypeStruct((points, k), cols.dtype),
        in_specs=[VMEM],
        out_specs=VMEM,
        compiler_params=params(8),
    )(cols)


def both(refs, rows, cols=slice(None), axis=1):
    return jnp.concatenate([r[rows, cols] for r in refs], axis=axis)


def first_sum(own, above, own_rows, above_rows):
    points, k = own.shape
    n = own_rows.shape[1]
    half = points // 2

    def kernel(own_ref, above_ref, own_rows_ref, above_rows_ref, sum_ref):
        for p in range(0, points, half):
            at = slice(p, p + half)
            left = both((own_ref, above_ref), at)
            for c in range(0, n, TILE):
                right = both(
                    (own_rows_ref, above_rows_ref), slice(None), slice(c, c + TILE), 0
                )
                sum_ref[at, c : c + TILE] = jnp.dot(
                    left, right, preferred_element_type=jnp.float32
                )

    return pl.pallas_call(
        kernel,
        out_shape=jax.ShapeDtypeStruct((points, n), jnp.float32),
        in_specs=[VMEM] * 4,
        out_specs=VMEM,
        compiler_params=params(12),
        cost_estimate=pl.CostEstimate(
            flops=4 * points * k * n, bytes_accessed=4 * points * n, transcendentals=0
        ),
    )(own, above, own_rows, above_rows)


def finished(total, below, upper, lower, below_rows, across_rows):
    points, k = below.shape
    n = below_rows.shape[1]
    tiles = [(h, c) for h in range(2) for c in range(0, n, TILE)]

    def kernel(
        total_ref, below_ref, upper_ref, lower_ref, below_rows_ref, across_rows_ref,
        out_ref, held, sems,
    ):
        copies = []
        for t, (h, c) in enumerate(tiles):
            at = (slice(0, CUT), slice(CUT, points))[h]
            where = (at, slice(c, c + TILE))
            left = jnp.concatenate(
                [below_ref[at, :], (upper_ref, lower_ref)[h][...]], axis=1
            )
            right = both((below_rows_ref, across_rows_ref), slice(None), where[1], 0)
            held[where] = (
                total_ref[where]
                + jnp.dot(left, right, preferred_element_type=jnp.float32)
            ).astype(jnp.bfloat16)
            copies.append(
                pltpu.make_async_copy(held.at[where], out_ref.at[where], sems.at[t])
            )
            copies[-1].start()
        for copy in copies:
            copy.wait()

    return pl.pallas_call(
        kernel,
        out_shape=jax.ShapeDtypeStruct((points, n), jnp.bfloat16),
        in_specs=[VMEM] * 6,
        out_specs=pl.BlockSpec(memory_space=pl.ANY),
        scratch_shapes=[
            pltpu.VMEM((points, n), jnp.bfloat16),
            pltpu.SemaphoreType.DMA((len(tiles),)),
        ],
        compiler_params=params(24),
        cost_estimate=pl.CostEstimate(
            flops=4 * points * k * n, bytes_accessed=6 * points * n, transcendentals=0
        ),
    )(total, below, upper, lower, below_rows, across_rows)


def from_band(block, offset):
    n = lax.axis_size(BAND)
    return lax.ppermute(block, BAND, [((i + offset) % n, i) for i in range(n)])


def on_device(orbitals, rotation):
    cols = orbitals.T
    width, n = cols.shape[0], rotation.shape[1]
    sent = copies_of(rotation, lax.axis_size(GRID))
    all_rows = lax.all_to_all(sent, GRID, 0, 0, tiled=True)
    all_rows = all_rows.reshape(-1, lax.axis_size(NEAR), width, n)
    near = lax.axis_index(NEAR)

    def rows(offset):
        which = lax.rem(near + offset, lax.axis_size(NEAR))
        return lax.dynamic_index_in_dim(all_rows, which, 1, False).reshape(-1, n)

    whole = turned(lax.all_gather(cols, FAR, axis=0, tiled=True))
    above = from_band(whole, 1)
    below = from_band(whole, -1)
    upper = from_band(above[:CUT], 1)
    lower = from_band(below[CUT:], -1)
    total = first_sum(whole, above, rows(0), rows(1))
    return finished(total, below, upper, lower, rows(3), rows(2))


def solution(mesh):
    n_grid, n_band = mesh.devices.shape
    fine = Mesh(
        mesh.devices.reshape(4, 4, n_grid // 16, n_band // 4, 4), (*GRID, *BAND)
    )
    spec = P(GRID, BAND)
    return jax.shard_map(
        on_device, mesh=fine, in_specs=(spec, spec), out_specs=spec, check_vma=False
    )
```

```python
import jax
import jax.numpy as jnp
from jax import lax
from jax.experimental import pallas as pl
from jax.experimental.pallas import tpu as pltpu
from jax.sharding import Mesh
from jax.sharding import PartitionSpec as P

GRID = ("x", "y", "core")
FAR, NEAR = "far", "near"
BAND = (FAR, NEAR)
VMEM = pl.BlockSpec(memory_space=pltpu.VMEM)
TILE = 512
CUT = 512


def params(mib):
    return pltpu.CompilerParams(vmem_limit_bytes=mib << 20)


def copies_of(block, n):
    held_n = n // 4

    def kernel(block_ref, out_ref, held, sems):
        value = block_ref[...]
        for i in range(held_n):
            held[i] = value
        copies = [
            pltpu.make_async_copy(
                held, out_ref.at[i * held_n : (i + 1) * held_n], sems.at[i]
            )
            for i in range(4)
        ]
        for copy in copies:
            copy.start()
        for copy in copies:
            copy.wait()

    return pl.pallas_call(
        kernel,
        out_shape=jax.ShapeDtypeStruct((n, *block.shape), block.dtype),
        in_specs=[VMEM],
        out_specs=pl.BlockSpec(memory_space=pltpu.HBM),
        scratch_shapes=[
            pltpu.VMEM((held_n, *block.shape), block.dtype),
            pltpu.SemaphoreType.DMA((4,)),
        ],
        compiler_params=params(4),
    )(block)


def turned(cols):
    k, points = cols.shape

    def kernel(cols_ref, out_ref):
        for i in range(0, points, 128):
            out_ref[i : i + 128, :] = cols_ref[:, i : i + 128].T

    return pl.pallas_call(
        kernel,
        out_shape=jax.ShapeDtypeStruct((points, k), cols.dtype),
        in_specs=[VMEM],
        out_specs=VMEM,
        compiler_params=params(8),
    )(cols)


def both(refs, rows, cols=slice(None), axis=1):
    return jnp.concatenate([r[rows, cols] for r in refs], axis=axis)


def first_sum(own, above, own_rows, above_rows):
    points, k = own.shape
    n = own_rows.shape[1]
    half = points // 2

    def kernel(own_ref, above_ref, own_rows_ref, above_rows_ref, sum_ref):
        for p in range(0, points, half):
            at = slice(p, p + half)
            left = both((own_ref, above_ref), at)
            for c in range(0, n, TILE):
                right = both(
                    (own_rows_ref, above_rows_ref), slice(None), slice(c, c + TILE), 0
                )
                sum_ref[at, c : c + TILE] = jnp.dot(
                    left, right, preferred_element_type=jnp.float32
                )

    return pl.pallas_call(
        kernel,
        out_shape=jax.ShapeDtypeStruct((points, n), jnp.float32),
        in_specs=[VMEM] * 4,
        out_specs=VMEM,
        compiler_params=params(12),
        cost_estimate=pl.CostEstimate(
            flops=4 * points * k * n, bytes_accessed=4 * points * n, transcendentals=0
        ),
    )(own, above, own_rows, above_rows)


def finished(total, below, across, below_rows, across_rows):
    points, k = below.shape
    n = below_rows.shape[1]
    tiles = [(h, c) for h in range(2) for c in range(0, n, TILE)]

    def kernel(
        total_ref, below_ref, across_ref, below_rows_ref, across_rows_ref,
        out_ref, held, sems,
    ):
        copies = []
        for t, (h, c) in enumerate(tiles):
            at = (slice(0, CUT), slice(CUT, points))[h]
            where = (at, slice(c, c + TILE))
            left = both((below_ref, across_ref), at)
            right = both((below_rows_ref, across_rows_ref), slice(None), where[1], 0)
            held[where] = (
                total_ref[where]
                + jnp.dot(left, right, preferred_element_type=jnp.float32)
            ).astype(jnp.bfloat16)
            copies.append(
                pltpu.make_async_copy(held.at[where], out_ref.at[where], sems.at[t])
            )
            copies[-1].start()
        for copy in copies:
            copy.wait()

    return pl.pallas_call(
        kernel,
        out_shape=jax.ShapeDtypeStruct((points, n), jnp.bfloat16),
        in_specs=[VMEM] * 5,
        out_specs=pl.BlockSpec(memory_space=pl.ANY),
        scratch_shapes=[
            pltpu.VMEM((points, n), jnp.bfloat16),
            pltpu.SemaphoreType.DMA((len(tiles),)),
        ],
        compiler_params=params(24),
        cost_estimate=pl.CostEstimate(
            flops=4 * points * k * n, bytes_accessed=6 * points * n, transcendentals=0
        ),
    )(total, below, across, below_rows, across_rows)


def from_band(block, offset):
    n = lax.axis_size(BAND)
    return lax.ppermute(block, BAND, [((i + offset) % n, i) for i in range(n)])


def on_device(orbitals, rotation):
    cols = orbitals.T
    width, n = cols.shape[0], rotation.shape[1]
    sent = copies_of(rotation, lax.axis_size(GRID))
    all_rows = lax.all_to_all(sent, GRID, 0, 0, tiled=True)
    all_rows = all_rows.reshape(-1, lax.axis_size(NEAR), width, n)
    near = lax.axis_index(NEAR)

    def rows(offset):
        which = lax.rem(near + offset, lax.axis_size(NEAR))
        return lax.dynamic_index_in_dim(all_rows, which, 1, False).reshape(-1, n)

    whole = turned(lax.all_gather(cols, FAR, axis=0, tiled=True))
    above = from_band(whole, 1)
    below = from_band(whole, -1)
    across = from_band(above, 1)
    total = first_sum(whole, below, rows(0), rows(3))
    return finished(total, above, across, rows(1), rows(2))


def solution(mesh):
    n_grid, n_band = mesh.devices.shape
    fine = Mesh(
        mesh.devices.reshape(4, 4, n_grid // 16, n_band // 4, 4), (*GRID, *BAND)
    )
    spec = P(GRID, BAND)
    return jax.shard_map(
        on_device, mesh=fine, in_specs=(spec, spec), out_specs=spec, check_vma=False
    )
```

```python
import jax
import jax.numpy as jnp
from jax import lax
from jax.experimental import pallas as pl
from jax.experimental.pallas import tpu as pltpu
from jax.sharding import Mesh
from jax.sharding import PartitionSpec as P

GRID = ("x", "y", "core")
FAR, NEAR = "far", "near"
BAND = (FAR, NEAR)
VMEM = pl.BlockSpec(memory_space=pltpu.VMEM)
TILE = 512
CUT = 512


def params(mib):
    return pltpu.CompilerParams(vmem_limit_bytes=mib << 20)


def copies_of(block, n):
    held_n = n // 4

    def kernel(block_ref, out_ref, held, sems):
        value = block_ref[...]
        for i in range(held_n):
            held[i] = value
        copies = [
            pltpu.make_async_copy(
                held, out_ref.at[i * held_n : (i + 1) * held_n], sems.at[i]
            )
            for i in range(4)
        ]
        for copy in copies:
            copy.start()
        for copy in copies:
            copy.wait()

    return pl.pallas_call(
        kernel,
        out_shape=jax.ShapeDtypeStruct((n, *block.shape), block.dtype),
        in_specs=[VMEM],
        out_specs=pl.BlockSpec(memory_space=pltpu.HBM),
        scratch_shapes=[
            pltpu.VMEM((held_n, *block.shape), block.dtype),
            pltpu.SemaphoreType.DMA((4,)),
        ],
        compiler_params=params(4),
    )(block)


def turned(cols):
    k, points = cols.shape

    def kernel(cols_ref, out_ref):
        for i in range(0, points, 128):
            out_ref[i : i + 128, :] = cols_ref[:, i : i + 128].T

    return pl.pallas_call(
        kernel,
        out_shape=jax.ShapeDtypeStruct((points, k), cols.dtype),
        in_specs=[VMEM],
        out_specs=VMEM,
        compiler_params=params(8),
    )(cols)


def both(refs, rows, cols=slice(None), axis=1):
    return jnp.concatenate([r[rows, cols] for r in refs], axis=axis)


def first_sum(parts, rows):
    points, k = parts[0].shape
    n, count = rows[0].shape[1], len(parts)
    half = points // 2

    def kernel(*refs):
        parts_refs, rows_refs, sum_ref = refs[:count], refs[count:-1], refs[-1]
        for p in range(0, points, half):
            at = slice(p, p + half)
            left = both(parts_refs, at)
            for c in range(0, n, TILE):
                right = both(rows_refs, slice(None), slice(c, c + TILE), 0)
                sum_ref[at, c : c + TILE] = jnp.dot(
                    left, right, preferred_element_type=jnp.float32
                )

    return pl.pallas_call(
        kernel,
        out_shape=jax.ShapeDtypeStruct((points, n), jnp.float32),
        in_specs=[VMEM] * (2 * count),
        out_specs=VMEM,
        compiler_params=params(12),
        cost_estimate=pl.CostEstimate(
            flops=6 * points * k * n, bytes_accessed=4 * points * n, transcendentals=0
        ),
    )(*parts, *rows)


def finished(total, across, across_rows):
    points, k = across.shape
    n = across_rows.shape[1]
    tiles = [(h, c) for h in range(2) for c in range(0, n, TILE)]

    def kernel(
        total_ref, across_ref, across_rows_ref, out_ref, held, sems
    ):
        copies = []
        for t, (h, c) in enumerate(tiles):
            at = (slice(0, CUT), slice(CUT, points))[h]
            where = (at, slice(c, c + TILE))
            left = across_ref[at, :]
            right = across_rows_ref[:, where[1]]
            held[where] = (
                total_ref[where]
                + jnp.dot(left, right, preferred_element_type=jnp.float32)
            ).astype(jnp.bfloat16)
            copies.append(
                pltpu.make_async_copy(held.at[where], out_ref.at[where], sems.at[t])
            )
            copies[-1].start()
        for copy in copies:
            copy.wait()

    return pl.pallas_call(
        kernel,
        out_shape=jax.ShapeDtypeStruct((points, n), jnp.bfloat16),
        in_specs=[VMEM] * 3,
        out_specs=pl.BlockSpec(memory_space=pl.ANY),
        scratch_shapes=[
            pltpu.VMEM((points, n), jnp.bfloat16),
            pltpu.SemaphoreType.DMA((len(tiles),)),
        ],
        compiler_params=params(24),
        cost_estimate=pl.CostEstimate(
            flops=4 * points * k * n, bytes_accessed=6 * points * n, transcendentals=0
        ),
    )(total, across, across_rows)


def from_band(block, offset):
    n = lax.axis_size(BAND)
    return lax.ppermute(block, BAND, [((i + offset) % n, i) for i in range(n)])


def on_device(orbitals, rotation):
    cols = orbitals.T
    width, n = cols.shape[0], rotation.shape[1]
    sent = copies_of(rotation, lax.axis_size(GRID))
    all_rows = lax.all_to_all(sent, GRID, 0, 0, tiled=True)
    all_rows = all_rows.reshape(-1, lax.axis_size(NEAR), width, n)
    near = lax.axis_index(NEAR)

    def rows(offset):
        which = lax.rem(near + offset, lax.axis_size(NEAR))
        return lax.dynamic_index_in_dim(all_rows, which, 1, False).reshape(-1, n)

    whole = turned(lax.all_gather(cols, FAR, axis=0, tiled=True))
    above = from_band(whole, 1)
    below = from_band(whole, -1)
    across = from_band(above, 1)
    total = first_sum((whole, below, above), (rows(0), rows(3), rows(1)))
    return finished(total, across, rows(2))


def solution(mesh):
    n_grid, n_band = mesh.devices.shape
    fine = Mesh(
        mesh.devices.reshape(4, 4, n_grid // 16, n_band // 4, 4), (*GRID, *BAND)
    )
    spec = P(GRID, BAND)
    return jax.shard_map(
        on_device, mesh=fine, in_specs=(spec, spec), out_specs=spec, check_vma=False
    )
```
